32 devices in a mesh: groups: 2 (over y), frame: 4 (over z), tok: 2 (over x), head: 2 (over core).
Axes of the slice: x: 2, y: 2, z: 4, core: 2. Of those that a mesh axis runs over, the one named last changes fastest.
Arguments:
- frames: bfloat16 [8, 1024, 1152], P(('groups', 'frame'), 'tok'), parts along dimension 0, may hold values from -6 to 6
- modulation: float32 [3, 1152], replicated, may hold values from -4.1 to 6, as said below
- w_qkv: bfloat16 [1152, 16, 3, 72], P('frame', 'head'), may hold values from -0.1875 to 0.1875
- w_out: bfloat16 [1152, 1152], P('head', 'frame'), may hold values from -0.1875 to 0.1875
- anchor_offsets: int32 [2], P('groups'), parts along dimension 0, may hold values from 0 to 3
Outputs:
- updated: bfloat16 [8, 1024, 1152], P(('groups', 'frame'), 'tok', 'head'), parts along dimension 0
The draws below stay inside these ranges and needn't reach their ends.
There are 2 independent parts, one for each index of `groups`. The reference program is written for one: setup_inputs(seed, part) draws one part's arguments, and reference() takes and returns one part's arrays. A program takes and returns all parts, laid end to end along the dimension named above; an argument that names none is the same for every part. Nothing has to cross between parts.
Inputs may be any that keep to these rules, and one draw needn't show every extreme that they name: anchor_offsets[c] is the offset, within span c of 4 frames, of the frame that all frames of the span attend to. `modulation`: row 0 is the shift, row 1 the scale, row 2 the gate.
All inputs are finite; a program needn't handle non-finite values.
Results may differ from the reference program's by a relative error of at most 0.0049.
The reference program's roundings to bfloat16 on the way count: a program that leaves them out, or rounds other values in their place, can miss the bound.
Values may be sent and summed in bfloat16 or wider, within the bound.
A program may use at most 64 MiB of HBM per device.

```python
import jax
import jax.numpy as jnp
from jax import lax

D = 1152
HEADS = 16
HD = 72
FTOK = 1024
FRAMES = 4
SPAN = 4
SPANS = 1


def draw_modulation(key, part):
    key_shift, key_scale, key_sign, key_gate = jax.random.split(jax.random.fold_in(key, 11), 4)
    shift_vec = jnp.clip(0.5 * jax.random.normal(key_shift, (D,), jnp.float32), -2.0, 2.0)
    scale_vec = jax.random.uniform(key_scale, (D,), jnp.float32, -0.5, 1.0)
    sign_vec = jnp.where(jax.random.bernoulli(key_sign, 0.5, (D,)), 1.0, -1.0)
    gate_vec = sign_vec * jnp.exp(jax.random.uniform(key_gate, (D,), jnp.float32, 0.0, 1.4))
    return jnp.stack([shift_vec, scale_vec, gate_vec]).astype(jnp.float32)


def block_scale(stream_key, dims, cuts, low, high):
    def one(position, shards_of):
        steps = jax.random.uniform(jax.random.fold_in(jax.random.fold_in(stream_key, 6), position), (shards_of,), jnp.float32, low / len(cuts), high / len(cuts))
        return jnp.repeat(jnp.exp(steps), dims[position] // shards_of).reshape((-1,) + (1,) * (len(dims) - position - 1))

    loudness = one(*cuts[0])
    for cut in cuts[1:]:
        loudness = loudness * one(*cut)
    return loudness


def bell_draw(own_key, extent, spread, most, cuts=(), held_as=jnp.bfloat16):
    level = block_scale(own_key, extent, cuts, -0.22, 0.18) if cuts else 1.0
    entries = jax.random.normal(own_key, extent, jnp.float32) * spread * level
    return jnp.minimum(jnp.maximum(entries, -most), most).astype(held_as)


def setup_inputs(seed: int = 0, part: int = 0) -> dict:
    keys = jax.random.split(jax.random.key(seed), 6)
    part_keys = jax.random.split(jax.random.fold_in(keys[5], part), 6)
    return {
        "frames": bell_draw(part_keys[0], (FRAMES, FTOK, D), 1.0, 6.0, ((0, 4), (1, 2))),
        "modulation": draw_modulation(jax.random.fold_in(keys[5], 71), part),
        "w_qkv": bell_draw(keys[2], (D, HEADS, 3, HD), D ** -0.5, 0.1875, ((0, 4), (1, 2))),
        "w_out": bell_draw(keys[3], (HEADS * HD, D), (HEADS * HD) ** -0.5, 0.1875, ((0, 2), (1, 4))),
        "anchor_offsets": jax.random.randint(part_keys[4], (SPANS,), 0, SPAN).astype(jnp.int32),
    }


def normalize(frame_data, modulation):
    values = frame_data.astype(jnp.float32)
    row_mean = lax.optimization_barrier(jnp.mean(values, axis=-1, keepdims=True))
    centred = values - row_mean
    row_var = lax.optimization_barrier(jnp.mean(centred * centred, axis=-1, keepdims=True))
    normed = centred * lax.rsqrt(row_var + 1e-06)
    return (normed * (1.0 + modulation[1]) + modulation[0]).astype(jnp.bfloat16)

def reference(frames, modulation, w_qkv, w_out, anchor_offsets):
    flat_weight = w_qkv.reshape(D, HEADS * 3 * HD)

    def project(frame_data):
        mixed = jnp.dot(normalize(frame_data, modulation), flat_weight, preferred_element_type=jnp.float32)
        return mixed.astype(jnp.bfloat16).reshape(FTOK, HEADS, 3, HD)

    def key_values(frame_data):
        mixed = project(frame_data)
        return (mixed[:, :, 1, :], mixed[:, :, 2, :])
    all_keys, all_vals = lax.map(key_values, frames)

    def one_frame(frame_idx):
        frame_data = frames[frame_idx]
        query = project(frame_data)[:, :, 0, :]
        span_idx = frame_idx // SPAN
        anchor = span_idx * SPAN + anchor_offsets[span_idx]
        prev_idx = jnp.maximum(frame_idx - 1, 0)
        key_rows = jnp.concatenate([all_keys[anchor], all_keys[prev_idx], all_keys[frame_idx]], 0)
        val_rows = jnp.concatenate([all_vals[anchor], all_vals[prev_idx], all_vals[frame_idx]], 0)
        use_prev = frame_idx > 0
        use_anchor = (anchor != frame_idx) & (anchor != frame_idx - 1)
        valid_keys = jnp.concatenate([jnp.broadcast_to(use_anchor, (FTOK,)), jnp.broadcast_to(use_prev, (FTOK,)), jnp.ones((FTOK,), bool)])
        scores = jnp.einsum('qhd,khd->hqk', query.astype(jnp.float32), key_rows.astype(jnp.float32)) * HD ** (-0.5)
        scores = jnp.where(valid_keys[None, None, :], scores, -1e+30)
        row_max = lax.optimization_barrier(jnp.max(scores, axis=-1, keepdims=True))
        probs = jnp.exp(scores - row_max)
        denominator = lax.optimization_barrier(jnp.sum(probs, axis=-1, keepdims=True))
        probs_b = probs.astype(jnp.bfloat16)
        numerator = jnp.einsum('hqk,khd->hqd', probs_b.astype(jnp.float32), val_rows.astype(jnp.float32))
        attended = (numerator / denominator).astype(jnp.bfloat16)
        attended = jnp.transpose(attended, (1, 0, 2)).reshape(FTOK, HEADS * HD)
        projected = jnp.dot(attended, w_out, preferred_element_type=jnp.float32)
        return (frame_data.astype(jnp.float32) + modulation[2] * projected).astype(jnp.bfloat16)
    return lax.map(one_frame, jnp.arange(FRAMES, dtype=jnp.int32))
```

```python
import functools
import math

import jax
import jax.numpy as jnp
from jax import lax
from jax.experimental import pallas as pl
from jax.experimental.pallas import tpu as pltpu
from jax.sharding import PartitionSpec as P


def shifted(block, axis, distance):
    devices = range(lax.axis_size(axis))
    route = [(i - distance, i) for i in devices if i - distance in devices]
    return lax.ppermute(block, axis, route)


def from_partner(block, axis, stride):
    count = lax.axis_size(axis)
    route = []
    for low in range(count):
        high = low | 1 << stride
        if high != low and high < count:
            route += [(low, high), (high, low)]
    return lax.ppermute(block, axis, route)


def attend(queries, kv_all, first_frame, anchor, head_dim):
    frame_count, query_rows, query_width = queries.shape
    key_count = kv_all.shape[1]
    head_count = query_width // head_dim
    block_rows = math.gcd(512, query_rows)
    kv_heads = kv_all.reshape(frame_count + 2, key_count, head_count, 2, head_dim)
    global_idx = first_frame + 0
    use_prev = global_idx > 0
    use_anchor = (anchor != global_idx) & (anchor != global_idx - 1)
    valid_keys = jnp.concatenate(
        [
            jnp.broadcast_to(use_anchor, (key_count,)),
            jnp.broadcast_to(use_prev, (key_count,)),
            jnp.ones((key_count,), bool),
        ]
    )
    frame_queries = queries[0]

    def one_head(head_idx):
        picked = lax.dynamic_index_in_dim(kv_heads, head_idx, 2, keepdims=False)
        key_rows = jnp.concatenate(
            [picked[frame_count + 1, :, 0], picked[frame_count, :, 0], picked[0, :, 0]], 0
        )
        val_rows = jnp.concatenate(
            [picked[frame_count + 1, :, 1], picked[frame_count, :, 1], picked[0, :, 1]], 0
        )
        query_head = lax.dynamic_slice_in_dim(frame_queries, head_idx * head_dim, head_dim, 1)
        query_blocks = query_head.reshape(query_rows // block_rows, block_rows, head_dim)

        def one_block(query_block):
            scores = lax.dot_general(
                query_block, key_rows, (((1,), (1,)), ((), ())), preferred_element_type=jnp.float32
            ) * head_dim ** (-0.5)
            scores = jnp.where(valid_keys[None, :], scores, -1e30)
            row_max = jnp.max(scores, axis=-1, keepdims=True)
            probs = jnp.exp(scores - row_max)
            denominator = jnp.sum(probs, axis=-1, keepdims=True)
            numerator = jnp.dot(
                probs.astype(jnp.bfloat16), val_rows, preferred_element_type=jnp.float32
            )
            return (numerator / denominator).astype(jnp.bfloat16)

        return lax.map(one_block, query_blocks).reshape(query_rows, head_dim)

    per_head = lax.map(one_head, jnp.arange(head_count, dtype=jnp.int32))
    frame_outputs = [jnp.transpose(per_head, (1, 0, 2)).reshape(query_rows, head_count * head_dim)]
    return jnp.stack(frame_outputs)


def on_device_rings(frames, modulation, w_qkv, w_out, anchor_offsets):
    frame_count, row_count, model_width = frames.shape
    head_local = w_qkv.shape[1]
    head_dim = w_qkv.shape[3]
    my_index = lax.axis_index("frame")
    flat_rows = frames.reshape(frame_count * row_count, model_width).astype(jnp.float32)
    row_mean = jnp.mean(flat_rows, axis=-1, keepdims=True)
    centred = flat_rows - row_mean
    row_var = jnp.mean(centred * centred, axis=-1, keepdims=True)
    normed = centred * lax.rsqrt(row_var + 1e-06)
    hidden = (normed * (1.0 + modulation[1]) + modulation[0]).astype(jnp.bfloat16)
    full_weight = lax.all_gather(w_qkv, "frame", axis=0, tiled=True)
    mixed = jnp.dot(
        hidden,
        full_weight.reshape(model_width, head_local * 3 * head_dim),
        preferred_element_type=jnp.float32,
    )
    mixed = mixed.astype(jnp.bfloat16).reshape(frame_count, row_count, head_local, 3, head_dim)
    queries = mixed[:, :, :, 0, :].reshape(frame_count, row_count, head_local * head_dim)
    keyvals = mixed[:, :, :, 1:, :].reshape(frame_count, row_count, head_local * 2 * head_dim)
    span_count = anchor_offsets.shape[0]
    total_frames = frame_count * lax.axis_size("frame")
    span_len = total_frames // span_count
    first_frame = my_index * frame_count
    mine_span = first_frame // span_len
    anchor = mine_span * span_len + anchor_offsets[mine_span]
    prev_kv = shifted(keyvals[frame_count - 1], "frame", 1)
    holder = anchor // frame_count
    anchor_kv = lax.dynamic_index_in_dim(keyvals, anchor % frame_count, 0, keepdims=False)
    levels = (span_len // frame_count).bit_length() - 1
    for bit_index in range(levels):
        partner = from_partner(anchor_kv, "frame", bit_index)
        take_partner = my_index >> bit_index & 1 != holder >> bit_index & 1
        anchor_kv = jnp.where(take_partner, partner, anchor_kv)
    kv_all = jnp.concatenate([keyvals, prev_kv[None], anchor_kv[None]], 0)
    kv_whole = lax.all_gather(kv_all, "tok", axis=1, tiled=True)
    attended = attend(queries, kv_whole, first_frame, anchor, head_dim)
    flat_attended = attended.reshape(frame_count * row_count, head_local * head_dim)
    term_cols = jnp.dot(
        flat_attended,
        lax.all_gather(w_out, "frame", axis=1, tiled=True),
        preferred_element_type=jnp.float32,
    )
    summed = lax.psum_scatter(term_cols, "head", scatter_dimension=1, tiled=True)
    half_width = summed.shape[1]
    col_start = lax.axis_index("head") * half_width
    residual_in = lax.dynamic_slice_in_dim(flat_rows, col_start, half_width, 1)
    gate_part = lax.dynamic_slice_in_dim(modulation[2], col_start, half_width, 0)
    result = (residual_in + gate_part * summed).astype(jnp.bfloat16)
    return result.reshape(frame_count, row_count, half_width)


MESH = pl.DeviceIdType.MESH


def remote(src, dst, send_sem, recv_sem, **where):
    return pltpu.make_async_remote_copy(
        src_ref=src,
        dst_ref=dst,
        send_sem=send_sem,
        recv_sem=recv_sem,
        device_id=where,
        device_id_type=MESH,
    )


def greet(peers):
    barrier = pltpu.get_barrier_semaphore()
    for peer in peers:
        pl.semaphore_signal(barrier, inc=1, device_id=peer, device_id_type=MESH)
    pl.semaphore_wait(barrier, len(peers))


def gather_kernel(
    nz, h_ref, w_ref, wo_ref, h_all, w_all, wo_all,
    local_sem, h_send, h_fwd, h_core, h_recv, w_send, w_fwd, w_recv, o_send, o_fwd, o_recv, o_own,
):
    y, z = lax.axis_index("groups"), lax.axis_index("frame")
    x, c = lax.axis_index("tok"), lax.axis_index("head")
    per_core = nz // 2
    quarter = h_ref.shape[0] // 2
    home = z // per_core
    slot = z % per_core
    others = [lax.rem(z + step, nz) for step in range(1, nz)]

    locals_ = [
        pltpu.make_async_copy(h_ref, h_all.at[z, pl.ds(x * 2 * quarter, 2 * quarter)], local_sem.at[0]),
        pltpu.make_async_copy(w_ref, w_all.at[z], local_sem.at[1]),
    ]
    for copy in locals_:
        copy.start()
    own_out = pltpu.make_async_copy(wo_ref, wo_all.at[slot, c], local_sem.at[2])

    @pl.when(home == c)
    def _():
        own_out.start()

    greet(
        [{"frame": other, "head": core} for other in others for core in (0, 1)]
        + [{"head": 1 - c}, {"tok": 1 - x}, {"groups": 1 - y}]
    )

    def piece(frame, tok, core):
        return h_all.at[frame, pl.ds((tok * 2 + core) * quarter, quarter)]

    mine = h_ref.at[pl.ds(c * quarter, quarter)]
    sends = []
    for k, other in enumerate(others):
        sends.append(remote(mine, piece(z, x, c), h_send.at[k], h_recv.at[z, x, c], frame=other))
        sends[-1].start()
    sends.append(remote(mine, piece(z, x, c), h_send.at[nz - 1], h_recv.at[z, x, c], tok=1 - x))
    sends[-1].start()
    for k, other in enumerate(others):
        sends.append(remote(w_ref.at[y], w_all.at[z, y], w_send.at[k], w_recv.at[z, y], frame=other))
        sends[-1].start()
    for k, other in enumerate(others):
        sends.append(
            remote(wo_ref.at[y], wo_all.at[slot, c, y], o_send.at[k], o_recv.at[slot, c, y], frame=other, head=home)
        )
        sends[-1].start()
    over = remote(wo_ref, wo_all.at[slot, c], o_send.at[nz - 1], o_own, head=1 - c)

    @pl.when(home != c)
    def _():
        over.start()

    def arrived(ref, sem):
        remote(ref, ref, h_send.at[0], sem, head=1 - c).wait_recv()

    for k, other in enumerate(others):
        got = piece(other, x, c)
        arrived(got, h_recv.at[other, x, c])
        sends.append(remote(got, got, h_fwd.at[k], h_recv.at[other, x, c], tok=1 - x))
        sends[-1].start()
        sends.append(remote(got, got, h_core.at[0, k], h_recv.at[other, x, c], head=1 - c))
        sends[-1].start()
        part = w_all.at[other, y]
        arrived(part, w_recv.at[other, y])
        sends.append(remote(part, part, w_fwd.at[k], w_recv.at[other, y], groups=1 - y))
        sends[-1].start()
    for i in range(per_core):
        for core in (0, 1):
            block = wo_all.at[i, core, y]
            onward = remote(block, block, o_fwd.at[i, core], o_recv.at[i, core, y], groups=1 - y)

            @pl.when(c * per_core + i != z)
            def _():
                arrived(block, o_recv.at[i, core, y])
                onward.start()

    for k, frame in enumerate([z] + others):
        got = piece(frame, 1 - x, c)
        arrived(got, h_recv.at[frame, 1 - x, c])
        sends.append(remote(got, got, h_core.at[1, k], h_recv.at[frame, 1 - x, c], head=1 - c))
        sends[-1].start()
    for other in others:
        arrived(w_all.at[other, 1 - y], w_recv.at[other, 1 - y])
        arrived(piece(other, x, 1 - c), h_recv.at[other, x, 1 - c])
    for frame in [z] + others:
        arrived(piece(frame, 1 - x, 1 - c), h_recv.at[frame, 1 - x, 1 - c])
    for i in range(per_core):
        for core in (0, 1):
            block = wo_all.at[i, core, y]
            onward = remote(block, block, o_fwd.at[i, core], o_recv.at[i, core, y], groups=1 - y)

            @pl.when(c * per_core + i != z)
            def _():
                arrived(wo_all.at[i, core, 1 - y], o_recv.at[i, core, 1 - y])
                onward.wait_send()

    @pl.when(home == c)
    def _():
        arrived(wo_all.at[slot, 1 - c], o_own)
        own_out.wait()

    @pl.when(home != c)
    def _():
        over.wait_send()

    for copy in locals_:
        copy.wait()
    for copy in sends:
        copy.wait_send()


def gather(hidden, weight, out_weight, nz):
    rows, width = hidden.shape
    dma = pltpu.SemaphoreType.DMA
    vmem, anywhere = pl.BlockSpec(memory_space=pltpu.VMEM), pl.BlockSpec(memory_space=pl.ANY)
    return pl.pallas_call(
        functools.partial(gather_kernel, nz),
        out_shape=(
            jax.ShapeDtypeStruct((nz, 2 * rows, width), hidden.dtype),
            jax.ShapeDtypeStruct((nz,) + weight.shape, weight.dtype),
            jax.ShapeDtypeStruct((nz // 2, 2) + out_weight.shape, out_weight.dtype),
        ),
        in_specs=[vmem] * 3,
        out_specs=(anywhere,) * 3,
        scratch_shapes=[
            dma((3,)),
            dma((nz,)),
            dma((nz - 1,)),
            dma((2, nz)),
            dma((nz, 2, 2)),
            dma((nz - 1,)),
            dma((nz - 1,)),
            dma((nz, 2)),
            dma((nz,)),
            dma((nz // 2, 2)),
            dma((nz // 2, 2, 2)),
            dma,
        ],
        compiler_params=pltpu.CompilerParams(collective_id=0, has_side_effects=True),
        name="gather",
    )(hidden, weight, out_weight)


def attend_kernel(heads, hd, chunk, pick, anc_ref, prev_ref, own_ref, w_ref, o_ref, wide, keys, vals, queries):
    step = pl.program_id(0)
    frame_rows = own_ref.shape[1]
    lanes = keys.shape[2]

    @pl.when(step == 0)
    def _():
        wide[...] = jnp.zeros_like(wide)
        for head in range(heads):
            for what in range(3):
                place = ((what + 2) % 3 * heads + head) * lanes
                wide[:, place : place + hd] = w_ref[:, (head * 3 + what) * hd : (head * 3 + what + 1) * hd]

        def project(ref, at, columns, targets, base):
            here = pl.ds(pl.multiple_of(at * chunk, chunk), chunk)
            there = pl.ds(pl.multiple_of(base + at * chunk, chunk), chunk)
            mixed = jnp.dot(ref[0, here, :], wide[:, columns], preferred_element_type=jnp.float32)
            mixed = mixed.astype(jnp.bfloat16)
            for t, target in enumerate(targets):
                for head in range(heads):
                    place = (t * heads + head) * lanes
                    target[head, there, :] = mixed[:, place : place + lanes]

        both = slice(0, 2 * heads * lanes)
        for block, ref in enumerate((anc_ref, prev_ref, own_ref)):

            @pl.loop(0, frame_rows // chunk)
            def _(at):
                project(ref, at, both, (keys, vals), block * frame_rows)

        @pl.loop(0, frame_rows // chunk)
        def _(at):
            project(own_ref, at, slice(2 * heads * lanes, 3 * heads * lanes), (queries,), 0)

    rate = hd ** (-0.5) * math.log2(math.e)
    offsets = [jnp.where(pick[3 + k] == 1, 0.0, -1e30).astype(jnp.float32) for k in range(2)] + [0.0]
    rows = o_ref.shape[0]
    here = pl.ds(pl.multiple_of(step * rows, rows), rows)
    for head in range(heads):
        query = queries[head, here, :]
        scores = [
            lax.dot_general(
                query,
                keys[head, k * frame_rows : (k + 1) * frame_rows, :],
                (((1,), (1,)), ((), ())),
                preferred_element_type=jnp.float32,
            )
            for k in range(3)
        ]
        tops = [jnp.max(s, axis=-1, keepdims=True) + offset for s, offset in zip(scores, offsets)]
        top = jnp.maximum(jnp.maximum(tops[0], tops[1]), tops[2])
        denominator, numerator = 0.0, 0.0
        for k in range(3):
            probs = jnp.exp2((scores[k] - (top - offsets[k])) * rate)
            denominator += jnp.sum(probs, axis=-1, keepdims=True)
            numerator += jnp.dot(
                probs.astype(jnp.bfloat16),
                vals[head, k * frame_rows : (k + 1) * frame_rows, :],
                preferred_element_type=jnp.float32,
            )
        result = (numerator / denominator).astype(jnp.bfloat16)
        o_ref[:, head * hd : (head + 1) * hd] = result[:, :hd]


def attend_heads(pick, h_all, weight, heads, hd):
    _, frame_rows, width = h_all.shape
    lanes = -(-hd // 128) * 128
    block_rows = math.gcd(256, frame_rows)

    def frame_block(which):
        return pl.BlockSpec((1, frame_rows, width), lambda i, pick: (pick[which], 0, 0))

    return pl.pallas_call(
        functools.partial(attend_kernel, heads, hd, block_rows),
        out_shape=jax.ShapeDtypeStruct((frame_rows, heads * hd), jnp.bfloat16),
        grid_spec=pltpu.PrefetchScalarGridSpec(
            num_scalar_prefetch=1,
            grid=(frame_rows // block_rows,),
            in_specs=[frame_block(2), frame_block(1), frame_block(0), pl.BlockSpec(weight.shape, lambda i, pick: (0, 0))],
            out_specs=pl.BlockSpec((block_rows, heads * hd), lambda i, pick: (i, 0)),
            scratch_shapes=[
                pltpu.VMEM((width, 3 * heads * lanes), jnp.bfloat16),
                pltpu.VMEM((heads, 3 * frame_rows, lanes), jnp.bfloat16),
                pltpu.VMEM((heads, 3 * frame_rows, lanes), jnp.bfloat16),
                pltpu.VMEM((heads, frame_rows, lanes), jnp.bfloat16),
            ],
        ),
        compiler_params=pltpu.CompilerParams(vmem_limit_bytes=56 * 1024 * 1024),
        name="attend",
    )(pick, h_all, h_all, h_all, weight)


def output_kernel(per_core, att_ref, wo_ref, res_ref, gate_ref, o_ref, held, send, recv):
    x, c = lax.axis_index("tok"), lax.axis_index("head")
    rows = o_ref.shape[0]
    greet([{"tok": 1 - x}, {"head": 1 - c}])
    mine = att_ref.at[pl.ds(pl.multiple_of(x * rows, rows), rows)]
    theirs = att_ref.at[pl.ds(pl.multiple_of((1 - x) * rows, rows), rows)]
    across = remote(theirs, held.at[0], send.at[0], recv.at[0], tok=1 - x)
    beside = remote(mine, held.at[1], send.at[1], recv.at[1], head=1 - c)
    relay = remote(held.at[0], held.at[2], send.at[2], recv.at[2], head=1 - c)
    across.start()
    beside.start()

    def term(block, core, tok):
        return [
            jnp.dot(block, wo_ref[i, core, tok], preferred_element_type=jnp.float32) for i in range(per_core)
        ]

    def plus(a, b):
        return [p + q for p, q in zip(a, b)]

    total = term(att_ref[pl.ds(pl.multiple_of(x * rows, rows), rows), :], c, x)
    beside.wait_recv()
    total = plus(total, term(held[1], 1 - c, x))
    across.wait_recv()
    relay.start()
    total = plus(total, term(held[0], c, 1 - x))
    relay.wait_recv()
    total = plus(total, term(held[2], 1 - c, 1 - x))
    width = wo_ref.shape[-1]
    for i in range(per_core):
        columns = slice(i * width, (i + 1) * width)
        o_ref[:, columns] = (res_ref[:, columns].astype(jnp.float32) + gate_ref[:, columns] * total[i]).astype(o_ref.dtype)
    across.wait_send()
    beside.wait_send()
    relay.wait_send()


def project_out(attended, out_weight, residual, gate):
    rows, columns = residual.shape
    dma = pltpu.SemaphoreType.DMA
    return pl.pallas_call(
        functools.partial(output_kernel, out_weight.shape[0]),
        out_shape=jax.ShapeDtypeStruct((rows, columns), jnp.bfloat16),
        in_specs=[pl.BlockSpec(memory_space=pltpu.VMEM)] * 4,
        out_specs=pl.BlockSpec(memory_space=pltpu.VMEM),
        scratch_shapes=[pltpu.VMEM((3, rows, attended.shape[1]), jnp.bfloat16), dma((3,)), dma((3,))],
        compiler_params=pltpu.CompilerParams(collective_id=1, has_side_effects=True),
        name="project_out",
    )(attended, out_weight, residual, gate)


def on_device(frames, modulation, w_qkv, w_out, anchor_offsets, mesh_shape):
    frame_count, row_count, model_width = frames.shape
    depth, head_local, _, head_dim = w_qkv.shape
    nz = mesh_shape["frame"]
    pairs = all(mesh_shape[axis] == 2 for axis in ("groups", "tok", "head"))
    if not (pairs and frame_count == 1 and anchor_offsets.shape[0] == 1 and nz % 2 == 0 and nz <= 4):
        return on_device_rings(frames, modulation, w_qkv, w_out, anchor_offsets)
    z, x, c = lax.axis_index("frame"), lax.axis_index("tok"), lax.axis_index("head")
    rows = frames[0]
    values = rows.astype(jnp.float32)
    row_mean = jnp.mean(values, axis=-1, keepdims=True)
    centred = values - row_mean
    row_var = jnp.mean(centred * centred, axis=-1, keepdims=True)
    normed = centred * lax.rsqrt(row_var + 1e-06)
    hidden = (normed * (1.0 + modulation[1]) + modulation[0]).astype(jnp.bfloat16)
    heads = head_local // 2
    weight = lax.dynamic_slice_in_dim(w_qkv, x * heads, heads, 1)
    weight = weight.reshape(2, depth // 2, heads * 3 * head_dim)
    out_weight = w_out.reshape(2, w_out.shape[0] // 2, w_out.shape[1])
    h_all, w_all, wo_all = gather(hidden, weight, out_weight, nz)
    anchor = anchor_offsets[0]
    pick = jnp.stack(
        [
            z,
            jnp.maximum(z - 1, 0),
            anchor,
            ((anchor != z) & (anchor != z - 1)).astype(jnp.int32),
            (z > 0).astype(jnp.int32),
        ]
    ).astype(jnp.int32)
    attended = attend_heads(pick, h_all, w_all.reshape(model_width, heads * 3 * head_dim), heads, head_dim)
    half_width = model_width // 2
    residual = lax.dynamic_slice_in_dim(rows, c * half_width, half_width, 1)
    gate = lax.dynamic_slice_in_dim(modulation[2:3], c * half_width, half_width, 1)
    return project_out(attended, wo_all, residual, gate)[None]


def solution(mesh):
    placed = (
        P(("groups", "frame"), "tok", None),
        P(),
        P("frame", "head", None, None),
        P("head", "frame"),
        P("groups"),
    )
    return jax.shard_map(
        functools.partial(on_device, mesh_shape=dict(mesh.shape)),
        mesh=mesh,
        in_specs=placed,
        out_specs=P(("groups", "frame"), "tok", "head"),
        check_vma=False,
    )
```

```python
import functools
import math

import jax
import jax.numpy as jnp
from jax import lax
from jax.experimental import pallas as pl
from jax.experimental.pallas import tpu as pltpu
from jax.sharding import PartitionSpec as P


def shifted(block, axis, distance):
    devices = range(lax.axis_size(axis))
    route = [(i - distance, i) for i in devices if i - distance in devices]
    return lax.ppermute(block, axis, route)


def from_partner(block, axis, stride):
    count = lax.axis_size(axis)
    route = []
    for low in range(count):
        high = low | 1 << stride
        if high != low and high < count:
            route += [(low, high), (high, low)]
    return lax.ppermute(block, axis, route)


def attend(queries, kv_all, first_frame, anchor, head_dim):
    frame_count, query_rows, query_width = queries.shape
    key_count = kv_all.shape[1]
    head_count = query_width // head_dim
    block_rows = math.gcd(512, query_rows)
    kv_heads = kv_all.reshape(frame_count + 2, key_count, head_count, 2, head_dim)
    global_idx = first_frame + 0
    use_prev = global_idx > 0
    use_anchor = (anchor != global_idx) & (anchor != global_idx - 1)
    valid_keys = jnp.concatenate(
        [
            jnp.broadcast_to(use_anchor, (key_count,)),
            jnp.broadcast_to(use_prev, (key_count,)),
            jnp.ones((key_count,), bool),
        ]
    )
    frame_queries = queries[0]

    def one_head(head_idx):
        picked = lax.dynamic_index_in_dim(kv_heads, head_idx, 2, keepdims=False)
        key_rows = jnp.concatenate(
            [picked[frame_count + 1, :, 0], picked[frame_count, :, 0], picked[0, :, 0]], 0
        )
        val_rows = jnp.concatenate(
            [picked[frame_count + 1, :, 1], picked[frame_count, :, 1], picked[0, :, 1]], 0
        )
        query_head = lax.dynamic_slice_in_dim(frame_queries, head_idx * head_dim, head_dim, 1)
        query_blocks = query_head.reshape(query_rows // block_rows, block_rows, head_dim)

        def one_block(query_block):
            scores = lax.dot_general(
                query_block, key_rows, (((1,), (1,)), ((), ())), preferred_element_type=jnp.float32
            ) * head_dim ** (-0.5)
            scores = jnp.where(valid_keys[None, :], scores, -1e30)
            row_max = jnp.max(scores, axis=-1, keepdims=True)
            probs = jnp.exp(scores - row_max)
            denominator = jnp.sum(probs, axis=-1, keepdims=True)
            numerator = jnp.dot(
                probs.astype(jnp.bfloat16), val_rows, preferred_element_type=jnp.float32
            )
            return (numerator / denominator).astype(jnp.bfloat16)

        return lax.map(one_block, query_blocks).reshape(query_rows, head_dim)

    per_head = lax.map(one_head, jnp.arange(head_count, dtype=jnp.int32))
    frame_outputs = [jnp.transpose(per_head, (1, 0, 2)).reshape(query_rows, head_count * head_dim)]
    return jnp.stack(frame_outputs)


def on_device_rings(frames, modulation, w_qkv, w_out, anchor_offsets):
    frame_count, row_count, model_width = frames.shape
    head_local = w_qkv.shape[1]
    head_dim = w_qkv.shape[3]
    my_index = lax.axis_index("frame")
    flat_rows = frames.reshape(frame_count * row_count, model_width).astype(jnp.float32)
    row_mean = jnp.mean(flat_rows, axis=-1, keepdims=True)
    centred = flat_rows - row_mean
    row_var = jnp.mean(centred * centred, axis=-1, keepdims=True)
    normed = centred * lax.rsqrt(row_var + 1e-06)
    hidden = (normed * (1.0 + modulation[1]) + modulation[0]).astype(jnp.bfloat16)
    full_weight = lax.all_gather(w_qkv, "frame", axis=0, tiled=True)
    mixed = jnp.dot(
        hidden,
        full_weight.reshape(model_width, head_local * 3 * head_dim),
        preferred_element_type=jnp.float32,
    )
    mixed = mixed.astype(jnp.bfloat16).reshape(frame_count, row_count, head_local, 3, head_dim)
    queries = mixed[:, :, :, 0, :].reshape(frame_count, row_count, head_local * head_dim)
    keyvals = mixed[:, :, :, 1:, :].reshape(frame_count, row_count, head_local * 2 * head_dim)
    span_count = anchor_offsets.shape[0]
    total_frames = frame_count * lax.axis_size("frame")
    span_len = total_frames // span_count
    first_frame = my_index * frame_count
    mine_span = first_frame // span_len
    anchor = mine_span * span_len + anchor_offsets[mine_span]
    prev_kv = shifted(keyvals[frame_count - 1], "frame", 1)
    holder = anchor // frame_count
    anchor_kv = lax.dynamic_index_in_dim(keyvals, anchor % frame_count, 0, keepdims=False)
    levels = (span_len // frame_count).bit_length() - 1
    for bit_index in range(levels):
        partner = from_partner(anchor_kv, "frame", bit_index)
        take_partner = my_index >> bit_index & 1 != holder >> bit_index & 1
        anchor_kv = jnp.where(take_partner, partner, anchor_kv)
    kv_all = jnp.concatenate([keyvals, prev_kv[None], anchor_kv[None]], 0)
    kv_whole = lax.all_gather(kv_all, "tok", axis=1, tiled=True)
    attended = attend(queries, kv_whole, first_frame, anchor, head_dim)
    flat_attended = attended.reshape(frame_count * row_count, head_local * head_dim)
    term_cols = jnp.dot(
        flat_attended,
        lax.all_gather(w_out, "frame", axis=1, tiled=True),
        preferred_element_type=jnp.float32,
    )
    summed = lax.psum_scatter(term_cols, "head", scatter_dimension=1, tiled=True)
    half_width = summed.shape[1]
    col_start = lax.axis_index("head") * half_width
    residual_in = lax.dynamic_slice_in_dim(flat_rows, col_start, half_width, 1)
    gate_part = lax.dynamic_slice_in_dim(modulation[2], col_start, half_width, 0)
    result = (residual_in + gate_part * summed).astype(jnp.bfloat16)
    return result.reshape(frame_count, row_count, half_width)


MESH = pl.DeviceIdType.MESH


def remote(src, dst, send_sem, recv_sem, **where):
    return pltpu.make_async_remote_copy(
        src_ref=src,
        dst_ref=dst,
        send_sem=send_sem,
        recv_sem=recv_sem,
        device_id=where,
        device_id_type=MESH,
    )


def greet(peers):
    barrier = pltpu.get_barrier_semaphore()
    for peer in peers:
        pl.semaphore_signal(barrier, inc=1, device_id=peer, device_id_type=MESH)
    pl.semaphore_wait(barrier, len(peers))


def gather_kernel(
    nz, h_ref, w_ref, wo_ref, h_all, w_all, wo_all,
    local_sem, h_send, h_line, h_fwd, h_core, h_tok, h_tok_own, h_recv, w_send, w_line, w_fwd, w_recv,
    o_send, o_fwd, o_recv, o_own,
):
    y, z = lax.axis_index("groups"), lax.axis_index("frame")
    x, c = lax.axis_index("tok"), lax.axis_index("head")
    per_core = nz // 2
    quarter = h_ref.shape[0] // 2
    home = z // per_core
    slot = z % per_core
    others = [lax.rem(z + step, nz) for step in range(1, nz)]

    locals_ = [
        pltpu.make_async_copy(h_ref, h_all.at[z, pl.ds(x * 2 * quarter, 2 * quarter)], local_sem.at[0]),
        pltpu.make_async_copy(w_ref, w_all.at[z], local_sem.at[1]),
    ]
    for copy in locals_:
        copy.start()
    own_out = pltpu.make_async_copy(wo_ref, wo_all.at[slot, c], local_sem.at[2])

    @pl.when(home == c)
    def _():
        own_out.start()

    greet(
        [{"frame": other, "head": core} for other in others for core in (0, 1)]
        + [{"head": 1 - c}, {"tok": 1 - x}, {"groups": 1 - y}]
    )

    def piece(frame, tok, core):
        return h_all.at[frame, pl.ds((tok * 2 + core) * quarter, quarter)]

    def each_source(visit):
        for d in range(1, nz):
            for side, sign in enumerate((-1, 1)):
                source = z + sign * d

                @pl.when((source >= 0) & (source < nz))
                def _():
                    visit(source, (side, d - 1), z - sign)

    def if_inside(frame, act):
        @pl.when((frame >= 0) & (frame < nz))
        def _():
            act()

    mine = h_ref.at[pl.ds(c * quarter, quarter)]
    out = remote(mine, piece(z, x, c), h_send.at[2], h_recv.at[z, x, c], tok=1 - x)

    def first(side, sign):
        return (
            remote(mine, piece(z, x, c), h_send.at[side], h_recv.at[z, x, c], frame=z + sign),
            remote(w_ref.at[y], w_all.at[z, y], w_send.at[side], w_recv.at[z, y], frame=z + sign),
        )

    def onward_h(source, at, ahead):
        got = piece(source, x, c)
        return remote(got, got, h_line.at[at], h_recv.at[source, x, c], frame=ahead)

    def onward_w(source, at, ahead):
        got = w_all.at[source, y]
        return remote(got, got, w_line.at[at], w_recv.at[source, y], frame=ahead)

    def across_h(source, at):
        got = piece(source, x, c)
        return (
            remote(got, got, h_fwd.at[at], h_recv.at[source, x, c], tok=1 - x),
            remote(got, got, h_core.at[at], h_recv.at[source, x, c], head=1 - c),
        )

    def across_w(source, at):
        got = w_all.at[source, y]
        return remote(got, got, w_fwd.at[at], w_recv.at[source, y], groups=1 - y)

    def from_tok(source, sem):
        got = piece(source, 1 - x, c)
        return remote(got, got, sem, h_recv.at[source, 1 - x, c], head=1 - c)

    for side, sign in enumerate((-1, 1)):
        if_inside(z + sign, lambda: [copy.start() for copy in first(side, sign)])
    out.start()

    def arrived(ref, sem):
        remote(ref, ref, h_send.at[0], sem, head=1 - c).wait_recv()

    def pass_on(source, at, ahead):
        arrived(piece(source, x, c), h_recv.at[source, x, c])
        if_inside(ahead, lambda: onward_h(source, at, ahead).start())
        for copy in across_h(source, at):
            copy.start()
        arrived(w_all.at[source, y], w_recv.at[source, y])
        if_inside(ahead, lambda: onward_w(source, at, ahead).start())
        across_w(source, at).start()

    sends = []
    for k, other in enumerate(others):
        sends.append(
            remote(wo_ref.at[y], wo_all.at[slot, c, y], o_send.at[k], o_recv.at[slot, c, y], frame=other, head=home)
        )
        sends[-1].start()
    over = remote(wo_ref, wo_all.at[slot, c], o_send.at[nz - 1], o_own, head=1 - c)

    @pl.when(home != c)
    def _():
        over.start()

    each_source(pass_on)
    arrived(piece(z, 1 - x, c), h_recv.at[z, 1 - x, c])
    from_tok(z, h_tok_own).start()

    def pass_tok(source, at, ahead):
        arrived(piece(source, 1 - x, c), h_recv.at[source, 1 - x, c])
        from_tok(source, h_tok.at[at]).start()

    each_source(pass_tok)
    for i in range(per_core):
        for core in (0, 1):
            block = wo_all.at[i, core, y]
            onward = remote(block, block, o_fwd.at[i, core], o_recv.at[i, core, y], groups=1 - y)

            @pl.when(c * per_core + i != z)
            def _():
                arrived(block, o_recv.at[i, core, y])
                onward.start()

    for other in others:
        arrived(w_all.at[other, 1 - y], w_recv.at[other, 1 - y])
        arrived(piece(other, x, 1 - c), h_recv.at[other, x, 1 - c])
    for frame in [z] + others:
        arrived(piece(frame, 1 - x, 1 - c), h_recv.at[frame, 1 - x, 1 - c])
    for i in range(per_core):
        for core in (0, 1):
            block = wo_all.at[i, core, y]
            onward = remote(block, block, o_fwd.at[i, core], o_recv.at[i, core, y], groups=1 - y)

            @pl.when(c * per_core + i != z)
            def _():
                arrived(wo_all.at[i, core, 1 - y], o_recv.at[i, core, 1 - y])
                onward.wait_send()

    @pl.when(home == c)
    def _():
        arrived(wo_all.at[slot, 1 - c], o_own)
        own_out.wait()

    @pl.when(home != c)
    def _():
        over.wait_send()

    for side, sign in enumerate((-1, 1)):
        if_inside(z + sign, lambda: [copy.wait_send() for copy in first(side, sign)])
    out.wait_send()
    from_tok(z, h_tok_own).wait_send()

    def finish(source, at, ahead):
        if_inside(ahead, lambda: onward_h(source, at, ahead).wait_send())
        if_inside(ahead, lambda: onward_w(source, at, ahead).wait_send())
        for copy in across_h(source, at):
            copy.wait_send()
        across_w(source, at).wait_send()
        from_tok(source, h_tok.at[at]).wait_send()

    each_source(finish)
    for copy in locals_:
        copy.wait()
    for copy in sends:
        copy.wait_send()


def gather(hidden, weight, out_weight, nz):
    rows, width = hidden.shape
    dma = pltpu.SemaphoreType.DMA
    vmem, anywhere = pl.BlockSpec(memory_space=pltpu.VMEM), pl.BlockSpec(memory_space=pl.ANY)
    return pl.pallas_call(
        functools.partial(gather_kernel, nz),
        out_shape=(
            jax.ShapeDtypeStruct((nz, 2 * rows, width), hidden.dtype),
            jax.ShapeDtypeStruct((nz,) + weight.shape, weight.dtype),
            jax.ShapeDtypeStruct((nz // 2, 2) + out_weight.shape, out_weight.dtype),
        ),
        in_specs=[vmem] * 3,
        out_specs=(anywhere,) * 3,
        scratch_shapes=[
            dma((3,)),
            dma((3,)),
            dma((2, nz - 1)),
            dma((2, nz - 1)),
            dma((2, nz - 1)),
            dma((2, nz - 1)),
            dma,
            dma((nz, 2, 2)),
            dma((2,)),
            dma((2, nz - 1)),
            dma((2, nz - 1)),
            dma((nz, 2)),
            dma((nz,)),
            dma((nz // 2, 2)),
            dma((nz // 2, 2, 2)),
            dma,
        ],
        compiler_params=pltpu.CompilerParams(collective_id=0, has_side_effects=True),
        name="gather",
    )(hidden, weight, out_weight)


def attend_kernel(heads, hd, chunk, pick, anc_ref, prev_ref, own_ref, w_ref, o_ref, wide, keys, vals, queries):
    step = pl.program_id(0)
    frame_rows = own_ref.shape[1]
    lanes, depth = keys.shape[2], w_ref.shape[2]

    @pl.when(step == 0)
    def _():
        wide[...] = jnp.zeros_like(wide)
        for head in range(heads):
            for what in range(3):
                place = ((what + 2) % 3 * heads + head) * lanes
                for part in range(w_ref.shape[0]):
                    wide[place : place + hd, part * depth : (part + 1) * depth] = w_ref[
                        part, (head * 3 + what) * hd : (head * 3 + what + 1) * hd, :
                    ]

        def project(ref, at, columns, targets, base):
            here = pl.ds(pl.multiple_of(at * chunk, chunk), chunk)
            there = pl.ds(pl.multiple_of(base + at * chunk, chunk), chunk)
            mixed = lax.dot_general(
                ref[0, here, :], wide[columns, :], (((1,), (1,)), ((), ())), preferred_element_type=jnp.float32
            )
            mixed = mixed.astype(jnp.bfloat16)
            for t, target in enumerate(targets):
                for head in range(heads):
                    place = (t * heads + head) * lanes
                    target[head, there, :] = mixed[:, place : place + lanes]

        both = slice(0, 2 * heads * lanes)
        for block, ref in enumerate((anc_ref, prev_ref, own_ref)):

            @pl.loop(0, frame_rows // chunk)
            def _(at):
                project(ref, at, both, (keys, vals), block * frame_rows)

        @pl.loop(0, frame_rows // chunk)
        def _(at):
            project(own_ref, at, slice(2 * heads * lanes, 3 * heads * lanes), (queries,), 0)

    rate = hd ** (-0.5) * math.log2(math.e)
    offsets = [jnp.where(pick[3 + k] == 1, 0.0, -1e30).astype(jnp.float32) for k in range(2)] + [0.0]
    rows = o_ref.shape[0]
    here = pl.ds(pl.multiple_of(step * rows, rows), rows)
    for head in range(heads):
        query = queries[head, here, :]
        scores = [
            lax.dot_general(
                query,
                keys[head, k * frame_rows : (k + 1) * frame_rows, :],
                (((1,), (1,)), ((), ())),
                preferred_element_type=jnp.float32,
            )
            for k in range(3)
        ]
        tops = [jnp.max(s, axis=-1, keepdims=True) + offset for s, offset in zip(scores, offsets)]
        top = jnp.maximum(jnp.maximum(tops[0], tops[1]), tops[2])
        denominator, numerator = 0.0, 0.0
        for k in range(3):
            probs = jnp.exp2((scores[k] - (top - offsets[k])) * rate)
            denominator += jnp.sum(probs, axis=-1, keepdims=True)
            numerator += jnp.dot(
                probs.astype(jnp.bfloat16),
                vals[head, k * frame_rows : (k + 1) * frame_rows, :],
                preferred_element_type=jnp.float32,
            )
        result = (numerator / denominator).astype(jnp.bfloat16)
        o_ref[:, head * hd : (head + 1) * hd] = result[:, :hd]


def attend_heads(pick, h_all, weight, heads, hd):
    _, frame_rows, width = h_all.shape
    lanes = -(-hd // 128) * 128
    block_rows = math.gcd(256, frame_rows)

    def frame_block(which):
        return pl.BlockSpec((1, frame_rows, width), lambda i, pick: (pick[which], 0, 0))

    return pl.pallas_call(
        functools.partial(attend_kernel, heads, hd, block_rows),
        out_shape=jax.ShapeDtypeStruct((frame_rows, heads * hd), jnp.bfloat16),
        grid_spec=pltpu.PrefetchScalarGridSpec(
            num_scalar_prefetch=1,
            grid=(frame_rows // block_rows,),
            in_specs=[frame_block(2), frame_block(1), frame_block(0), pl.BlockSpec(weight.shape, lambda i, pick: (0, 0, 0))],
            out_specs=pl.BlockSpec((block_rows, heads * hd), lambda i, pick: (i, 0)),
            scratch_shapes=[
                pltpu.VMEM((3 * heads * lanes, width), jnp.bfloat16),
                pltpu.VMEM((heads, 3 * frame_rows, lanes), jnp.bfloat16),
                pltpu.VMEM((heads, 3 * frame_rows, lanes), jnp.bfloat16),
                pltpu.VMEM((heads, frame_rows, lanes), jnp.bfloat16),
            ],
        ),
        compiler_params=pltpu.CompilerParams(vmem_limit_bytes=56 * 1024 * 1024),
        name="attend",
    )(pick, h_all, h_all, h_all, weight)


def output_kernel(per_core, att_ref, wo_ref, res_ref, gate_ref, o_ref, held, send, recv):
    x, c = lax.axis_index("tok"), lax.axis_index("head")
    rows = o_ref.shape[0]
    greet([{"tok": 1 - x}, {"head": 1 - c}])
    mine = att_ref.at[pl.ds(pl.multiple_of(x * rows, rows), rows)]
    theirs = att_ref.at[pl.ds(pl.multiple_of((1 - x) * rows, rows), rows)]
    across = remote(theirs, held.at[0], send.at[0], recv.at[0], tok=1 - x)
    beside = remote(mine, held.at[1], send.at[1], recv.at[1], head=1 - c)
    relay = remote(held.at[0], held.at[2], send.at[2], recv.at[2], head=1 - c)
    across.start()
    beside.start()

    def term(block, core, tok):
        return [
            jnp.dot(block, wo_ref[i, core, tok], preferred_element_type=jnp.float32) for i in range(per_core)
        ]

    def plus(a, b):
        return [p + q for p, q in zip(a, b)]

    total = term(att_ref[pl.ds(pl.multiple_of(x * rows, rows), rows), :], c, x)
    beside.wait_recv()
    total = plus(total, term(held[1], 1 - c, x))
    across.wait_recv()
    relay.start()
    total = plus(total, term(held[0], c, 1 - x))
    relay.wait_recv()
    total = plus(total, term(held[2], 1 - c, 1 - x))
    width = wo_ref.shape[-1]
    for i in range(per_core):
        columns = slice(i * width, (i + 1) * width)
        o_ref[:, columns] = (res_ref[:, columns].astype(jnp.float32) + gate_ref[:, columns] * total[i]).astype(o_ref.dtype)
    across.wait_send()
    beside.wait_send()
    relay.wait_send()


def project_out(attended, out_weight, residual, gate):
    rows, columns = residual.shape
    dma = pltpu.SemaphoreType.DMA
    return pl.pallas_call(
        functools.partial(output_kernel, out_weight.shape[0]),
        out_shape=jax.ShapeDtypeStruct((rows, columns), jnp.bfloat16),
        in_specs=[pl.BlockSpec(memory_space=pltpu.VMEM)] * 4,
        out_specs=pl.BlockSpec(memory_space=pltpu.VMEM),
        scratch_shapes=[pltpu.VMEM((3, rows, attended.shape[1]), jnp.bfloat16), dma((3,)), dma((3,))],
        compiler_params=pltpu.CompilerParams(collective_id=1, has_side_effects=True),
        name="project_out",
    )(attended, out_weight, residual, gate)


def on_device(frames, modulation, w_qkv, w_out, anchor_offsets, mesh_shape):
    frame_count, row_count, model_width = frames.shape
    depth, head_local, _, head_dim = w_qkv.shape
    nz = mesh_shape["frame"]
    pairs = all(mesh_shape[axis] == 2 for axis in ("groups", "tok", "head"))
    if not (pairs and frame_count == 1 and anchor_offsets.shape[0] == 1 and nz % 2 == 0 and nz <= 4):
        return on_device_rings(frames, modulation, w_qkv, w_out, anchor_offsets)
    z, x, c = lax.axis_index("frame"), lax.axis_index("tok"), lax.axis_index("head")
    rows = frames[0]
    values = rows.astype(jnp.float32)
    row_mean = jnp.mean(values, axis=-1, keepdims=True)
    centred = values - row_mean
    row_var = jnp.mean(centred * centred, axis=-1, keepdims=True)
    normed = centred * lax.rsqrt(row_var + 1e-06)
    hidden = (normed * (1.0 + modulation[1]) + modulation[0]).astype(jnp.bfloat16)
    heads = head_local // 2
    weight = lax.dynamic_slice_in_dim(jnp.transpose(w_qkv, (1, 2, 3, 0)), x * heads, heads, 0)
    weight = weight.reshape(2, heads * 3 * head_dim // 2, depth)
    out_weight = w_out.reshape(2, w_out.shape[0] // 2, w_out.shape[1])
    h_all, w_all, wo_all = gather(hidden, weight, out_weight, nz)
    anchor = anchor_offsets[0]
    pick = jnp.stack(
        [
            z,
            jnp.maximum(z - 1, 0),
            anchor,
            ((anchor != z) & (anchor != z - 1)).astype(jnp.int32),
            (z > 0).astype(jnp.int32),
        ]
    ).astype(jnp.int32)
    attended = attend_heads(pick, h_all, w_all.reshape(nz, heads * 3 * head_dim, depth), heads, head_dim)
    half_width = model_width // 2
    residual = lax.dynamic_slice_in_dim(rows, c * half_width, half_width, 1)
    gate = lax.dynamic_slice_in_dim(modulation[2:3], c * half_width, half_width, 1)
    return project_out(attended, wo_all, residual, gate)[None]


def solution(mesh):
    placed = (
        P(("groups", "frame"), "tok", None),
        P(),
        P("frame", "head", None, None),
        P("head", "frame"),
        P("groups"),
    )
    return jax.shard_map(
        functools.partial(on_device, mesh_shape=dict(mesh.shape)),
        mesh=mesh,
        in_specs=placed,
        out_specs=P(("groups", "frame"), "tok", "head"),
        check_vma=False,
    )
```

```python
import functools
import math

import jax
import jax.numpy as jnp
from jax import lax
from jax.experimental import pallas as pl
from jax.experimental.pallas import tpu as pltpu
from jax.sharding import PartitionSpec as P


def shifted(block, axis, distance):
    devices = range(lax.axis_size(axis))
    route = [(i - distance, i) for i in devices if i - distance in devices]
    return lax.ppermute(block, axis, route)


def from_partner(block, axis, stride):
    count = lax.axis_size(axis)
    route = []
    for low in range(count):
        high = low | 1 << stride
        if high != low and high < count:
            route += [(low, high), (high, low)]
    return lax.ppermute(block, axis, route)


def attend(queries, kv_all, first_frame, anchor, head_dim):
    frame_count, query_rows, query_width = queries.shape
    key_count = kv_all.shape[1]
    head_count = query_width // head_dim
    block_rows = math.gcd(512, query_rows)
    kv_heads = kv_all.reshape(frame_count + 2, key_count, head_count, 2, head_dim)
    global_idx = first_frame + 0
    use_prev = global_idx > 0
    use_anchor = (anchor != global_idx) & (anchor != global_idx - 1)
    valid_keys = jnp.concatenate(
        [
            jnp.broadcast_to(use_anchor, (key_count,)),
            jnp.broadcast_to(use_prev, (key_count,)),
            jnp.ones((key_count,), bool),
        ]
    )
    frame_queries = queries[0]

    def one_head(head_idx):
        picked = lax.dynamic_index_in_dim(kv_heads, head_idx, 2, keepdims=False)
        key_rows = jnp.concatenate(
            [picked[frame_count + 1, :, 0], picked[frame_count, :, 0], picked[0, :, 0]], 0
        )
        val_rows = jnp.concatenate(
            [picked[frame_count + 1, :, 1], picked[frame_count, :, 1], picked[0, :, 1]], 0
        )
        query_head = lax.dynamic_slice_in_dim(frame_queries, head_idx * head_dim, head_dim, 1)
        query_blocks = query_head.reshape(query_rows // block_rows, block_rows, head_dim)

        def one_block(query_block):
            scores = lax.dot_general(
                query_block, key_rows, (((1,), (1,)), ((), ())), preferred_element_type=jnp.float32
            ) * head_dim ** (-0.5)
            scores = jnp.where(valid_keys[None, :], scores, -1e30)
            row_max = jnp.max(scores, axis=-1, keepdims=True)
            probs = jnp.exp(scores - row_max)
            denominator = jnp.sum(probs, axis=-1, keepdims=True)
            numerator = jnp.dot(
                probs.astype(jnp.bfloat16), val_rows, preferred_element_type=jnp.float32
            )
            return (numerator / denominator).astype(jnp.bfloat16)

        return lax.map(one_block, query_blocks).reshape(query_rows, head_dim)

    per_head = lax.map(one_head, jnp.arange(head_count, dtype=jnp.int32))
    frame_outputs = [jnp.transpose(per_head, (1, 0, 2)).reshape(query_rows, head_count * head_dim)]
    return jnp.stack(frame_outputs)


def on_device_rings(frames, modulation, w_qkv, w_out, anchor_offsets):
    frame_count, row_count, model_width = frames.shape
    head_local = w_qkv.shape[1]
    head_dim = w_qkv.shape[3]
    my_index = lax.axis_index("frame")
    flat_rows = frames.reshape(frame_count * row_count, model_width).astype(jnp.float32)
    row_mean = jnp.mean(flat_rows, axis=-1, keepdims=True)
    centred = flat_rows - row_mean
    row_var = jnp.mean(centred * centred, axis=-1, keepdims=True)
    normed = centred * lax.rsqrt(row_var + 1e-06)
    hidden = (normed * (1.0 + modulation[1]) + modulation[0]).astype(jnp.bfloat16)
    full_weight = lax.all_gather(w_qkv, "frame", axis=0, tiled=True)
    mixed = jnp.dot(
        hidden,
        full_weight.reshape(model_width, head_local * 3 * head_dim),
        preferred_element_type=jnp.float32,
    )
    mixed = mixed.astype(jnp.bfloat16).reshape(frame_count, row_count, head_local, 3, head_dim)
    queries = mixed[:, :, :, 0, :].reshape(frame_count, row_count, head_local * head_dim)
    keyvals = mixed[:, :, :, 1:, :].reshape(frame_count, row_count, head_local * 2 * head_dim)
    span_count = anchor_offsets.shape[0]
    total_frames = frame_count * lax.axis_size("frame")
    span_len = total_frames // span_count
    first_frame = my_index * frame_count
    mine_span = first_frame // span_len
    anchor = mine_span * span_len + anchor_offsets[mine_span]
    prev_kv = shifted(keyvals[frame_count - 1], "frame", 1)
    holder = anchor // frame_count
    anchor_kv = lax.dynamic_index_in_dim(keyvals, anchor % frame_count, 0, keepdims=False)
    levels = (span_len // frame_count).bit_length() - 1
    for bit_index in range(levels):
        partner = from_partner(anchor_kv, "frame", bit_index)
        take_partner = my_index >> bit_index & 1 != holder >> bit_index & 1
        anchor_kv = jnp.where(take_partner, partner, anchor_kv)
    kv_all = jnp.concatenate([keyvals, prev_kv[None], anchor_kv[None]], 0)
    kv_whole = lax.all_gather(kv_all, "tok", axis=1, tiled=True)
    attended = attend(queries, kv_whole, first_frame, anchor, head_dim)
    flat_attended = attended.reshape(frame_count * row_count, head_local * head_dim)
    term_cols = jnp.dot(
        flat_attended,
        lax.all_gather(w_out, "frame", axis=1, tiled=True),
        preferred_element_type=jnp.float32,
    )
    summed = lax.psum_scatter(term_cols, "head", scatter_dimension=1, tiled=True)
    half_width = summed.shape[1]
    col_start = lax.axis_index("head") * half_width
    residual_in = lax.dynamic_slice_in_dim(flat_rows, col_start, half_width, 1)
    gate_part = lax.dynamic_slice_in_dim(modulation[2], col_start, half_width, 0)
    result = (residual_in + gate_part * summed).astype(jnp.bfloat16)
    return result.reshape(frame_count, row_count, half_width)


MESH = pl.DeviceIdType.MESH


def remote(src, dst, send_sem, recv_sem, **where):
    return pltpu.make_async_remote_copy(
        src_ref=src,
        dst_ref=dst,
        send_sem=send_sem,
        recv_sem=recv_sem,
        device_id=where,
        device_id_type=MESH,
    )


def greet(peers):
    barrier = pltpu.get_barrier_semaphore()
    for peer in peers:
        pl.semaphore_signal(barrier, inc=1, device_id=peer, device_id_type=MESH)
    pl.semaphore_wait(barrier, len(peers))


def gather_kernel(
    nz, heads, hd, h_ref, w_ref, wo_ref, queries, keys, vals, wo_all, h_all, w_all, wide,
    local_sem, h_send, h_line, h_fwd, h_core, h_tok, h_tok_own, h_recv, w_send, w_line, w_fwd, w_recv,
    o_send, o_fwd, o_recv, o_own,
):
    y, z = lax.axis_index("groups"), lax.axis_index("frame")
    x, c = lax.axis_index("tok"), lax.axis_index("head")
    per_core = nz // 2
    quarter = h_ref.shape[0] // 2
    home = z // per_core
    slot = z % per_core
    others = [lax.rem(z + step, nz) for step in range(1, nz)]

    locals_ = [
        pltpu.make_async_copy(h_ref, h_all.at[z, pl.ds(x * 2 * quarter, 2 * quarter)], local_sem.at[0]),
        pltpu.make_async_copy(w_ref, w_all.at[z], local_sem.at[1]),
    ]
    for copy in locals_:
        copy.start()
    own_out = pltpu.make_async_copy(wo_ref, wo_all.at[slot, c], local_sem.at[2])

    @pl.when(home == c)
    def _():
        own_out.start()

    greet(
        [{"frame": other, "head": core} for other in others for core in (0, 1)]
        + [{"head": 1 - c}, {"tok": 1 - x}, {"groups": 1 - y}]
    )

    def piece(frame, tok, core):
        return h_all.at[frame, pl.ds((tok * 2 + core) * quarter, quarter)]

    def each_source(visit, steps=range(1, nz)):
        for d in steps:
            for side, sign in enumerate((-1, 1)):
                source = z + sign * d

                @pl.when((source >= 0) & (source < nz))
                def _():
                    visit(source, (side, d - 1), z - sign)

    def if_inside(frame, act):
        @pl.when((frame >= 0) & (frame < nz))
        def _():
            act()

    mine = h_ref.at[pl.ds(c * quarter, quarter)]
    out = remote(mine, piece(z, x, c), h_send.at[2], h_recv.at[z, x, c], tok=1 - x)

    def first_h(side, sign):
        return remote(mine, piece(z, x, c), h_send.at[side], h_recv.at[z, x, c], frame=z + sign)

    def first_w(side, sign):
        return remote(w_ref.at[y], w_all.at[z, y], w_send.at[side], w_recv.at[z, y], frame=z + sign)

    def onward_h(source, at, ahead):
        got = piece(source, x, c)
        return remote(got, got, h_line.at[at], h_recv.at[source, x, c], frame=ahead)

    def onward_w(source, at, ahead):
        got = w_all.at[source, y]
        return remote(got, got, w_line.at[at], w_recv.at[source, y], frame=ahead)

    def across_h(source, at):
        got = piece(source, x, c)
        return (
            remote(got, got, h_fwd.at[at], h_recv.at[source, x, c], tok=1 - x),
            remote(got, got, h_core.at[at], h_recv.at[source, x, c], head=1 - c),
        )

    def across_w(source, at):
        got = w_all.at[source, y]
        return remote(got, got, w_fwd.at[at], w_recv.at[source, y], groups=1 - y)

    def from_tok(source, sem):
        got = piece(source, 1 - x, c)
        return remote(got, got, sem, h_recv.at[source, 1 - x, c], head=1 - c)

    def arrived(ref, sem):
        remote(ref, ref, h_send.at[0], sem, head=1 - c).wait_recv()

    def pass_h(source, at, ahead):
        arrived(piece(source, x, c), h_recv.at[source, x, c])
        if_inside(ahead, lambda: onward_h(source, at, ahead).start())
        for copy in across_h(source, at):
            copy.start()

    def pass_w(source, at, ahead):
        arrived(w_all.at[source, y], w_recv.at[source, y])
        if_inside(ahead, lambda: onward_w(source, at, ahead).start())
        across_w(source, at).start()

    def pass_tok(source, at, ahead):
        arrived(piece(source, 1 - x, c), h_recv.at[source, 1 - x, c])
        from_tok(source, h_tok.at[at]).start()

    sends = [
        remote(wo_ref.at[y], wo_all.at[slot, c, y], o_send.at[k], o_recv.at[slot, c, y], frame=other, head=home)
        for k, other in enumerate(others)
    ]
    over = remote(wo_ref, wo_all.at[slot, c], o_send.at[nz - 1], o_own, head=1 - c)

    lanes, depth, chunk = keys.shape[3], w_ref.shape[2], math.gcd(256, keys.shape[2])

    def project(frame, columns, targets):
        @pl.loop(0, h_all.shape[1] // chunk)
        def _(at):
            here = pl.ds(pl.multiple_of(at * chunk, chunk), chunk)
            mixed = lax.dot_general(
                h_all[frame, here, :], wide[columns, :], (((1,), (1,)), ((), ())), preferred_element_type=jnp.float32
            ).astype(jnp.bfloat16)
            for t, target in enumerate(targets):
                for head in range(heads):
                    place = (t * heads + head) * lanes
                    target[head, here, :] = mixed[:, place : place + lanes]

    both = slice(0, 2 * heads * lanes)

    def project_source(source, at, ahead):
        arrived(piece(source, x, 1 - c), h_recv.at[source, x, 1 - c])
        arrived(piece(source, 1 - x, 1 - c), h_recv.at[source, 1 - x, 1 - c])
        project(source, both, (keys.at[source], vals.at[source]))

    for side, sign in enumerate((-1, 1)):
        if_inside(z + sign, lambda: first_w(side, sign).start())
        if_inside(z + sign, lambda: first_h(side, sign).start())
    out.start()
    wide[...] = jnp.zeros_like(wide)
    for d in range(1, nz):
        each_source(pass_w, [d])
        if d < nz - 1 or d == 1:
            each_source(pass_h, [d])
        if d == 1:
            arrived(piece(z, 1 - x, c), h_recv.at[z, 1 - x, c])
            from_tok(z, h_tok_own).start()
        else:
            each_source(pass_tok, [d - 1])
    for other in others:
        arrived(w_all.at[other, 1 - y], w_recv.at[other, 1 - y])
    for copy in locals_:
        copy.wait()
    half = w_ref.shape[1]
    for head in range(heads):
        for what in range(3):
            place = ((what + 2) % 3 * heads + head) * lanes
            low = (head * 3 + what) * hd
            at, low = low // half, low % half
            for part in range(nz):
                wide[place : place + hd, part * depth : (part + 1) * depth] = w_all[part, at, low : low + hd, :]
    arrived(piece(z, 1 - x, 1 - c), h_recv.at[z, 1 - x, 1 - c])
    project(z, slice(2 * heads * lanes, 3 * heads * lanes), (queries,))
    for copy in sends:
        copy.start()

    @pl.when(home != c)
    def _():
        over.start()

    project(z, both, (keys.at[z], vals.at[z]))
    for d in range(1, nz - 2):
        each_source(project_source, [d])
    if nz > 2:
        each_source(pass_h, [nz - 1])
    for d in range(max(1, nz - 2), nz - 1):
        each_source(project_source, [d])
    each_source(pass_tok, [nz - 1])
    each_source(project_source, [nz - 1])
    for i in range(per_core):
        for core in (0, 1):
            block = wo_all.at[i, core, y]
            onward = remote(block, block, o_fwd.at[i, core], o_recv.at[i, core, y], groups=1 - y)

            @pl.when(c * per_core + i != z)
            def _():
                arrived(block, o_recv.at[i, core, y])
                onward.start()

    for i in range(per_core):
        for core in (0, 1):
            block = wo_all.at[i, core, y]
            onward = remote(block, block, o_fwd.at[i, core], o_recv.at[i, core, y], groups=1 - y)

            @pl.when(c * per_core + i != z)
            def _():
                arrived(wo_all.at[i, core, 1 - y], o_recv.at[i, core, 1 - y])
                onward.wait_send()

    @pl.when(home == c)
    def _():
        arrived(wo_all.at[slot, 1 - c], o_own)
        own_out.wait()

    @pl.when(home != c)
    def _():
        over.wait_send()

    for side, sign in enumerate((-1, 1)):
        if_inside(z + sign, lambda: first_h(side, sign).wait_send())
        if_inside(z + sign, lambda: first_w(side, sign).wait_send())
    out.wait_send()
    from_tok(z, h_tok_own).wait_send()

    def finish(source, at, ahead):
        if_inside(ahead, lambda: onward_h(source, at, ahead).wait_send())
        if_inside(ahead, lambda: onward_w(source, at, ahead).wait_send())
        for copy in across_h(source, at):
            copy.wait_send()
        across_w(source, at).wait_send()
        from_tok(source, h_tok.at[at]).wait_send()

    each_source(finish)
    for copy in sends:
        copy.wait_send()


def gather(hidden, weight, out_weight, nz, heads, hd):
    rows, width = hidden.shape
    lanes = -(-hd // 128) * 128
    dma = pltpu.SemaphoreType.DMA
    vmem, anywhere = pl.BlockSpec(memory_space=pltpu.VMEM), pl.BlockSpec(memory_space=pl.ANY)
    per_frame = jax.ShapeDtypeStruct((nz, heads, 2 * rows, lanes), hidden.dtype)
    return pl.pallas_call(
        functools.partial(gather_kernel, nz, heads, hd),
        out_shape=(
            jax.ShapeDtypeStruct((heads, 2 * rows, lanes), hidden.dtype),
            per_frame,
            per_frame,
            jax.ShapeDtypeStruct((nz // 2, 2) + out_weight.shape, out_weight.dtype),
        ),
        in_specs=[vmem] * 3,
        out_specs=(vmem, vmem, vmem, anywhere),
        scratch_shapes=[
            pltpu.VMEM((nz, 2 * rows, width), hidden.dtype),
            pltpu.VMEM((nz,) + weight.shape, weight.dtype),
            pltpu.VMEM((3 * heads * lanes, width), weight.dtype),
            dma((3,)),
            dma((3,)),
            dma((2, nz - 1)),
            dma((2, nz - 1)),
            dma((2, nz - 1)),
            dma((2, nz - 1)),
            dma,
            dma((nz, 2, 2)),
            dma((2,)),
            dma((2, nz - 1)),
            dma((2, nz - 1)),
            dma((nz, 2)),
            dma((nz,)),
            dma((nz // 2, 2)),
            dma((nz // 2, 2, 2)),
            dma,
        ],
        compiler_params=pltpu.CompilerParams(
            collective_id=0, has_side_effects=True, vmem_limit_bytes=56 * 1024 * 1024
        ),
        name="gather",
    )(hidden, weight, out_weight)


def attend_kernel(hd, pick, q_ref, ka_ref, kp_ref, ko_ref, va_ref, vp_ref, vo_ref, o_ref):
    keys, vals = (ka_ref, kp_ref, ko_ref), (va_ref, vp_ref, vo_ref)
    rate = hd ** (-0.5) * math.log2(math.e)
    offsets = [jnp.where(pick[3 + k] == 1, 0.0, -1e30).astype(jnp.float32) for k in range(2)] + [0.0]
    for head in range(q_ref.shape[0]):
        query = q_ref[head]
        scores = [
            lax.dot_general(
                query,
                keys[k][0, head],
                (((1,), (1,)), ((), ())),
                preferred_element_type=jnp.float32,
            )
            for k in range(3)
        ]
        tops = [jnp.max(s, axis=-1, keepdims=True) + offset for s, offset in zip(scores, offsets)]
        top = jnp.maximum(jnp.maximum(tops[0], tops[1]), tops[2])
        denominator, numerator = 0.0, 0.0
        for k in range(3):
            probs = jnp.exp2((scores[k] - (top - offsets[k])) * rate)
            denominator += jnp.sum(probs, axis=-1, keepdims=True)
            numerator += jnp.dot(
                probs.astype(jnp.bfloat16),
                vals[k][0, head],
                preferred_element_type=jnp.float32,
            )
        result = (numerator / denominator).astype(jnp.bfloat16)
        o_ref[:, head * hd : (head + 1) * hd] = result[:, :hd]


def attend_heads(pick, queries, keys, vals, hd):
    _, heads, frame_rows, lanes = keys.shape
    block_rows = math.gcd(256, frame_rows)

    def frame_block(which):
        return pl.BlockSpec((1, heads, frame_rows, lanes), lambda i, pick: (pick[which], 0, 0, 0))

    blocks = [frame_block(which) for which in (2, 1, 0)]
    return pl.pallas_call(
        functools.partial(attend_kernel, hd),
        out_shape=jax.ShapeDtypeStruct((frame_rows, heads * hd), jnp.bfloat16),
        grid_spec=pltpu.PrefetchScalarGridSpec(
            num_scalar_prefetch=1,
            grid=(frame_rows // block_rows,),
            in_specs=[pl.BlockSpec((heads, block_rows, lanes), lambda i, pick: (0, i, 0))] + blocks * 2,
            out_specs=pl.BlockSpec((block_rows, heads * hd), lambda i, pick: (i, 0)),
        ),
        compiler_params=pltpu.CompilerParams(vmem_limit_bytes=48 * 1024 * 1024),
        name="attend",
    )(pick, queries, keys, keys, keys, vals, vals, vals)


def output_kernel(per_core, att_ref, wo_ref, res_ref, gate_ref, o_ref, held, send, recv):
    x, c = lax.axis_index("tok"), lax.axis_index("head")
    rows = o_ref.shape[0]
    greet([{"tok": 1 - x}, {"head": 1 - c}])
    mine = att_ref.at[pl.ds(pl.multiple_of(x * rows, rows), rows)]
    theirs = att_ref.at[pl.ds(pl.multiple_of((1 - x) * rows, rows), rows)]
    across = remote(theirs, held.at[0], send.at[0], recv.at[0], tok=1 - x)
    beside = remote(mine, held.at[1], send.at[1], recv.at[1], head=1 - c)
    relay = remote(held.at[0], held.at[2], send.at[2], recv.at[2], head=1 - c)
    across.start()
    beside.start()

    def term(block, core, tok):
        return [
            jnp.dot(block, wo_ref[i, core, tok], preferred_element_type=jnp.float32) for i in range(per_core)
        ]

    def plus(a, b):
        return [p + q for p, q in zip(a, b)]

    total = term(att_ref[pl.ds(pl.multiple_of(x * rows, rows), rows), :], c, x)
    beside.wait_recv()
    total = plus(total, term(held[1], 1 - c, x))
    across.wait_recv()
    relay.start()
    total = plus(total, term(held[0], c, 1 - x))
    relay.wait_recv()
    total = plus(total, term(held[2], 1 - c, 1 - x))
    width = wo_ref.shape[-1]
    for i in range(per_core):
        columns = slice(i * width, (i + 1) * width)
        o_ref[:, columns] = (res_ref[:, columns].astype(jnp.float32) + gate_ref[:, columns] * total[i]).astype(o_ref.dtype)
    across.wait_send()
    beside.wait_send()
    relay.wait_send()


def project_out(attended, out_weight, residual, gate):
    rows, columns = residual.shape
    dma = pltpu.SemaphoreType.DMA
    return pl.pallas_call(
        functools.partial(output_kernel, out_weight.shape[0]),
        out_shape=jax.ShapeDtypeStruct((rows, columns), jnp.bfloat16),
        in_specs=[pl.BlockSpec(memory_space=pltpu.VMEM)] * 4,
        out_specs=pl.BlockSpec(memory_space=pltpu.VMEM),
        scratch_shapes=[pltpu.VMEM((3, rows, attended.shape[1]), jnp.bfloat16), dma((3,)), dma((3,))],
        compiler_params=pltpu.CompilerParams(collective_id=1, has_side_effects=True),
        name="project_out",
    )(attended, out_weight, residual, gate)


def on_device(frames, modulation, w_qkv, w_out, anchor_offsets, mesh_shape):
    frame_count, row_count, model_width = frames.shape
    depth, head_local, _, head_dim = w_qkv.shape
    nz = mesh_shape["frame"]
    pairs = all(mesh_shape[axis] == 2 for axis in ("groups", "tok", "head"))
    if not (pairs and frame_count == 1 and anchor_offsets.shape[0] == 1 and nz % 2 == 0 and nz <= 4):
        return on_device_rings(frames, modulation, w_qkv, w_out, anchor_offsets)
    z, x, c = lax.axis_index("frame"), lax.axis_index("tok"), lax.axis_index("head")
    rows = frames[0]
    values = rows.astype(jnp.float32)
    row_mean = jnp.mean(values, axis=-1, keepdims=True)
    centred = values - row_mean
    row_var = jnp.mean(centred * centred, axis=-1, keepdims=True)
    normed = centred * lax.rsqrt(row_var + 1e-06)
    hidden = (normed * (1.0 + modulation[1]) + modulation[0]).astype(jnp.bfloat16)
    heads = head_local // 2
    weight = lax.dynamic_slice_in_dim(jnp.transpose(w_qkv, (1, 2, 3, 0)), x * heads, heads, 0)
    weight = weight.reshape(2, heads * 3 * head_dim // 2, depth)
    out_weight = w_out.reshape(2, w_out.shape[0] // 2, w_out.shape[1])
    queries, keys, vals, wo_all = gather(hidden, weight, out_weight, nz, heads, head_dim)
    anchor = anchor_offsets[0]
    pick = jnp.stack(
        [
            z,
            jnp.maximum(z - 1, 0),
            anchor,
            ((anchor != z) & (anchor != z - 1)).astype(jnp.int32),
            (z > 0).astype(jnp.int32),
        ]
    ).astype(jnp.int32)
    attended = attend_heads(pick, queries, keys, vals, head_dim)
    half_width = model_width // 2
    residual = lax.dynamic_slice_in_dim(rows, c * half_width, half_width, 1)
    gate = lax.dynamic_slice_in_dim(modulation[2:3], c * half_width, half_width, 1)
    return project_out(attended, wo_all, residual, gate)[None]


def solution(mesh):
    placed = (
        P(("groups", "frame"), "tok", None),
        P(),
        P("frame", "head", None, None),
        P("head", "frame"),
        P("groups"),
    )
    return jax.shard_map(
        functools.partial(on_device, mesh_shape=dict(mesh.shape)),
        mesh=mesh,
        in_specs=placed,
        out_specs=P(("groups", "frame"), "tok", "head"),
        check_vma=False,
    )
```
